32 devices in a mesh: dp: 8 (over z, x), tensor: 4 (over y, core).
Axes of the slice: x: 2, y: 2, z: 4, core: 2. Of those that a mesh axis runs over, the one named last changes fastest.
Arguments:
- tokens: bfloat16 [32, 1024, 768], P(('dp', 'tensor')), may hold values from -6 to 6
- cotangent: bfloat16 [32, 1024, 768], P(('dp', 'tensor')), may hold values from -6 to 6
- span_start: int32 [32], P(('dp', 'tensor')), may hold values from 0 to 1023
- span_length: int32 [32], P(('dp', 'tensor')), may hold values from 1 to 512
- timestep: int32 [32], P(('dp', 'tensor')), may hold values from 0 to 999
- cond_table: float32 [1000, 128], replicated, may hold values from -6 to 6
- mask_embed: float32 [768], replicated, may hold values from -6 to 6
- ada_weight: float32 [128, 4608], replicated, may hold values from -0.5 to 0.5
- ada_bias: float32 [4608], replicated, may hold values from -3 to 3
- first_gain: float32 [768], replicated, may hold values from 0.25 to 1.75
- qkv_weight: bfloat16 [768, 2304], P(None, 'tensor'), may hold values from -0.21875 to 0.21875
- out_weight: bfloat16 [768, 768], P('tensor'), may hold values from -2.5 to 2.5
- second_gain: float32 [768], replicated, may hold values from 0.25 to 1.75
- up_weight: bfloat16 [768, 3072], P(None, 'tensor'), may hold values from -0.21875 to 0.21875
- up_bias: bfloat16 [3072], P('tensor'), may hold values from -3 to 3
- down_weight: bfloat16 [3072, 768], P('tensor'), may hold values from -0.109375 to 0.109375
- down_bias: bfloat16 [768], replicated, may hold values from -3 to 3
Outputs:
- layer_out: bfloat16 [32, 1024, 768], P(('dp', 'tensor'))
- tokens_grad: float32 [32, 1024, 768], P(('dp', 'tensor'))
- table_grad: float32 [1000, 128], replicated
- mask_grad: float32 [768], replicated
- ada_weight_grad: float32 [128, 4608], replicated
- ada_bias_grad: float32 [4608], replicated
- first_gain_grad: float32 [768], replicated
- qkv_grad: float32 [768, 2304], P(None, 'tensor')
- out_grad: float32 [768, 768], P('tensor')
- second_gain_grad: float32 [768], replicated
- up_grad: float32 [768, 3072], P(None, 'tensor')
- up_bias_grad: float32 [3072], P('tensor')
- down_grad: float32 [3072, 768], P('tensor')
- down_bias_grad: float32 [768], replicated
The draws below stay inside these ranges and needn't reach their ends.
All inputs are finite; a program needn't handle non-finite values.
Results may differ from the reference program's by a relative error of at most 0.0095.
The reference program's roundings to bfloat16 on the way count: a program that leaves them out, or rounds other values in their place, can miss the bound.
Values may be sent and summed in bfloat16 or wider, within the bound.
No kernel may reach another device: no remote copies, remote signals or barrier semaphores. Data moves between devices by JAX's collectives and lax.ppermute only.
A program may use at most 256 MiB of HBM per device.

```python
import math
import jax
import jax.numpy as jnp
from jax import lax

D = 768
HEAD_DIM = 64
FF = 3072
COND = 128
NSTEPS = 1000
SEQ_LEN = 1024
SEQS = 32


def plant(array, own_key, smallest, largest):
    dims = array.shape
    place = [jax.random.randint(jax.random.fold_in(own_key, axis), (), 0, dims[axis]) for axis in range(len(dims))]
    array = array.at[tuple(place)].set(smallest)
    longest = dims.index(max(dims))
    place[longest] = (place[longest] + 1) % dims[longest]
    return array.at[tuple(place)].set(largest)


def block_scale(own_key, extent, cuts, smallest, high):
    def one(dim, parts):
        draws = jax.random.uniform(jax.random.fold_in(jax.random.fold_in(own_key, 6), dim), (parts,), jnp.float32, smallest / len(cuts), high / len(cuts))
        return jnp.repeat(jnp.exp(draws), extent[dim] // parts).reshape((-1,) + (1,) * (len(extent) - dim - 1))

    gain = one(*cuts[0])
    for cut in cuts[1:]:
        gain = gain * one(*cut)
    return gain


def scatter_about(key, shape, width, limit, cuts=(), kind=jnp.bfloat16):
    level = block_scale(key, shape, cuts, -0.22, 0.18) if cuts else 1.0
    entries = jax.random.normal(key, shape, jnp.float32) * width * level
    return jnp.minimum(jnp.maximum(entries, -limit), limit).astype(kind)


def setup_inputs(seed: int = 0) -> dict:
    splits = jax.random.split(jax.random.key(seed), 18)
    return {
        "tokens": scatter_about(splits[0], (SEQS, SEQ_LEN, D), 1.0, 6.0, ((0, 32),)),
        "cotangent": scatter_about(splits[1], (SEQS, SEQ_LEN, D), 1.0, 6.0, ((0, 32),)),
        "span_start": plant(jax.random.randint(splits[2], (SEQS,), 0, SEQ_LEN), jax.random.fold_in(splits[2], 1), 0, SEQ_LEN - 1).astype(jnp.int32),
        "span_length": plant(jax.random.randint(splits[3], (SEQS,), 1, SEQ_LEN // 2 + 1), jax.random.fold_in(splits[3], 1), 1, (SEQ_LEN // 2 + 1) - 1).astype(jnp.int32),
        "timestep": plant(jax.random.randint(splits[4], (SEQS,), 0, NSTEPS), jax.random.fold_in(splits[4], 1), 0, NSTEPS - 1).astype(jnp.int32),
        "cond_table": scatter_about(splits[5], (NSTEPS, COND), 1.0, 6.0, (), jnp.float32),
        "mask_embed": scatter_about(splits[6], (D,), 1.0, 6.0, (), jnp.float32),
        "ada_weight": scatter_about(splits[7], (COND, 6 * D), COND ** -0.5, 0.5, (), jnp.float32),
        "ada_bias": scatter_about(splits[8], (6 * D,), 0.5, 3.0, (), jnp.float32),
        "first_gain": jnp.clip(1.0 + 0.15 * jax.random.normal(splits[9], (D,), jnp.float32), 0.25, 1.75),
        "qkv_weight": scatter_about(splits[10], (D, 3 * D), D ** -0.5, 0.21875, ((1, 4),)),
        "out_weight": scatter_about(splits[11], (D, D), (max(1, D * 8 // SEQ_LEN)) ** -0.5, 2.5, ((0, 4),)),
        "second_gain": jnp.clip(1.0 + 0.15 * jax.random.normal(splits[12], (D,), jnp.float32), 0.25, 1.75),
        "up_weight": scatter_about(splits[13], (D, FF), D ** -0.5, 0.21875, ((1, 4),)),
        "up_bias": scatter_about(splits[14], (FF,), 0.5, 3.0, ((0, 4),)),
        "down_weight": scatter_about(splits[15], (FF, D), FF ** -0.5, 0.109375, ((0, 4),)),
        "down_bias": scatter_about(splits[16], (D,), 0.5, 3.0),
    }


@jax.custom_vjp
def low(v):
    return lax.optimization_barrier(v.astype(jnp.bfloat16)).astype(jnp.float32)

@jax.custom_vjp
def low_back(v):
    return v

def low_keep(v):
    return (low(v), None)

def low_pass(kept, grad):
    return (grad,)

def back_keep(v):
    return (v, None)

def back_low(kept, grad):
    return (low(grad),)
low.defvjp(low_keep, low_pass)
low_back.defvjp(back_keep, back_low)
highest = lax.Precision.HIGHEST
epsilon = 1e-05

def matmul(left, right):
    return jnp.dot(left, right, precision=highest, preferred_element_type=jnp.float32)

def layer_norm(values, gain_vector):
    center = values - lax.optimization_barrier(jnp.mean(values, axis=-1, keepdims=True))
    variance = lax.optimization_barrier(jnp.mean(center * center, axis=-1, keepdims=True))
    return center * lax.rsqrt(variance + epsilon) * gain_vector

def modulate(values, gain_vector, shift_rows, scale_rows):
    return layer_norm(values, gain_vector) * (1.0 + scale_rows) + shift_rows

def rotary_tables(positions, head_width):
    half_width = head_width // 2
    frequency = jnp.exp(jnp.arange(half_width, dtype=jnp.float32) * (-2.0 * math.log(10000.0) / head_width))
    angles = positions.astype(jnp.float32)[:, None] * frequency[None, :]
    cosine = jnp.cos(angles)
    sine = jnp.sin(angles)
    return (jnp.concatenate([cosine, cosine], axis=1), jnp.concatenate([sine, sine], axis=1))

def rotate(values, cosine, sine):
    half_width = values.shape[-1] // 2
    turned = jnp.concatenate([-values[..., half_width:], values[..., :half_width]], axis=-1)
    return values * cosine[:, None, :] + turned * sine[:, None, :]

def sequence_layer(inputs, masked, onehot, cond_table, mask_embed, ada_weight, ada_bias, first_gain, qkv_weight, out_weight, second_gain, up_weight, up_bias, down_weight, down_bias):
    length, model_width = inputs.shape
    heads_count = model_width // HEAD_DIM
    score_scale = HEAD_DIM ** (-0.5)
    condition = jax.nn.silu(matmul(onehot[None, :], cond_table))
    modulation = matmul(condition, ada_weight) + ada_bias[None, :]
    shift_one, scale_one, gate_one, shift_two, scale_two, gate_two = jnp.split(modulation, 6, axis=1)
    start_rows = jnp.where(masked[:, None], mask_embed[None, :], inputs)
    first_low = low(modulate(start_rows, first_gain, shift_one, scale_one))
    projected = low_back(matmul(first_low, qkv_weight)).reshape(length, heads_count, 3, HEAD_DIM)
    cosine, sine = rotary_tables(jnp.arange(length, dtype=jnp.int32), HEAD_DIM)
    queries = low(rotate(projected[:, :, 0], cosine, sine))
    key_rows = low(rotate(projected[:, :, 1], cosine, sine))
    value_rows = low(projected[:, :, 2])
    scores = low_back(jnp.einsum('qhd,khd->hqk', queries, key_rows, precision=highest) * score_scale)
    weights_low = low(jax.nn.softmax(scores, axis=-1))
    mixed_rows = low_back(low(jnp.einsum('hqk,khd->qhd', weights_low, value_rows, precision=highest)))
    mixed_rows = mixed_rows.reshape(length, model_width)
    attention_out = low_back(matmul(mixed_rows, out_weight))
    middle = start_rows + gate_one * attention_out
    second_low = low(modulate(middle, second_gain, shift_two, scale_two))
    hidden_in = low_back(matmul(second_low, up_weight) + up_bias[None, :])
    hidden_low = low(jax.nn.gelu(hidden_in, approximate=True))
    feed_out = low_back(matmul(hidden_low, down_weight) + down_bias[None, :])
    return middle + gate_two * feed_out

def reference(tokens, cotangent, span_start, span_length, timestep, cond_table, mask_embed, ada_weight, ada_bias, first_gain, qkv_weight, out_weight, second_gain, up_weight, up_bias, down_weight, down_bias):
    params = tuple((weight_array.astype(jnp.float32) for weight_array in (cond_table, mask_embed, ada_weight, ada_bias, first_gain, qkv_weight, out_weight, second_gain, up_weight, up_bias, down_weight, down_bias)))
    positions = jnp.arange(SEQ_LEN, dtype=jnp.int32)
    step_ids = jnp.arange(NSTEPS, dtype=jnp.int32)

    def per_sequence(totals, element):
        inputs, upstream, span_first, span_size, step_index = element
        masked = (positions >= span_first) & (positions < span_first + span_size)
        onehot = (step_ids == step_index).astype(jnp.float32)

        def forward(values, *weights):
            return sequence_layer(values, masked, onehot, *weights)
        result, pullback = jax.vjp(forward, inputs.astype(jnp.float32), *params)
        gradients = pullback(upstream.astype(jnp.float32))
        totals = tuple((running + fresh for running, fresh in zip(totals, gradients[1:])))
        return (totals, (result.astype(jnp.bfloat16), gradients[0]))
    initial = tuple((jnp.zeros_like(weight_array) for weight_array in params))
    totals, (layer_out, tokens_grad) = lax.scan(per_sequence, initial, (tokens, cotangent, span_start, span_length, timestep))
    table_grad, mask_grad, ada_weight_grad, ada_bias_grad, first_gain_grad, qkv_grad, out_grad, second_gain_grad, up_grad, up_bias_grad, down_grad, down_bias_grad = totals
    return (layer_out, tokens_grad, table_grad, mask_grad, ada_weight_grad, ada_bias_grad, first_gain_grad, qkv_grad, out_grad, second_gain_grad, up_grad, up_bias_grad, down_grad, down_bias_grad)
```

```python
import functools
import math

import jax
import jax.numpy as jnp
from jax import lax
from jax.experimental import pallas as pl
from jax.experimental.pallas import tpu as pltpu
from jax.sharding import PartitionSpec as P

HEAD_DIM = 64
BF = jnp.bfloat16
F32 = jnp.float32
EPS = 1e-05
VMEM_LIMIT = 58 * 1024 * 1024


def nn(left, right):
    return lax.dot_general(left, right, (((1,), (0,)), ((), ())), preferred_element_type=F32)


def nt(left, right):
    return lax.dot_general(left, right, (((1,), (1,)), ((), ())), preferred_element_type=F32)


def tn(left, right):
    return lax.dot_general(left, right, (((0,), (0,)), ((), ())), preferred_element_type=F32)


def vmem():
    return pl.BlockSpec(memory_space=pltpu.VMEM)


def rotate(u, c, s):
    half = u.shape[0] // 2
    a, b = u[:half], u[half:]
    return jnp.concatenate([a * c - b * s, b * c + a * s], axis=0)


def rotate_back(w, c, s):
    half = w.shape[0] // 2
    a, b = w[:half], w[half:]
    return jnp.concatenate([a * c + b * s, b * c - a * s], axis=0)


def attend_forward_kernel(first, heads, block, *refs):
    if first:
        x, wqkv, wout, cos, sin, qkv, mixed, lse, total, keys = refs
    else:
        x, wqkv, wout, cos, sin, carried, qkv, mixed, lse, total, keys = refs
    hd = HEAD_DIM
    length = x.shape[0]

    def one_head(h, _):
        base = pl.multiple_of(h * 3 * hd, 3 * hd)
        projected = nt(wqkv[pl.ds(base, 3 * hd), :], x[...])
        c, s = cos[...], sin[...]
        qkv[pl.ds(base, hd), :] = rotate(projected[:hd], c, s).astype(BF) * BF(hd**-0.5)
        key = rotate(projected[hd : 2 * hd], c, s).astype(BF)
        qkv[pl.ds(base + hd, hd), :] = key
        qkv[pl.ds(base + 2 * hd, hd), :] = projected[2 * hd :].astype(BF)
        keys[...] = key.T
        for b in range(length // block):
            cols = slice(b * block, (b + 1) * block)
            scores = nn(keys[...], qkv[pl.ds(base, hd), cols])
            top = jnp.max(scores, axis=0, keepdims=True)
            power = jnp.exp(scores - top)
            norm = jnp.sum(power, axis=0, keepdims=True)
            probs = (power * (1.0 / norm)).astype(BF)
            out = nn(qkv[pl.ds(base + 2 * hd, hd), :], probs)
            mixed[pl.ds(pl.multiple_of(h * hd, hd), hd), cols] = out.astype(BF)
            lse[pl.ds(pl.multiple_of(h * 8, 8), 8), cols] = jnp.broadcast_to(
                top + jnp.log(norm), (8, block)
            )
        return 0

    lax.fori_loop(0, heads, one_head, 0)
    part = tn(mixed[...], wout[: heads * hd, :])
    total[...] = part if first else carried[...] + part


def attend_forward(x, wqkv, wout, cos, sin, carried):
    length, width = x.shape
    heads = wqkv.shape[0] // (3 * HEAD_DIM)
    block = min(256, length)
    first = carried is None
    args = (x, wqkv, wout, cos, sin) + (() if first else (carried,))
    return pl.pallas_call(
        functools.partial(attend_forward_kernel, first, heads, block),
        out_shape=(
            jax.ShapeDtypeStruct((3 * heads * HEAD_DIM, length), BF),
            jax.ShapeDtypeStruct((heads * HEAD_DIM, length), BF),
            jax.ShapeDtypeStruct((heads * 8, length), F32),
            jax.ShapeDtypeStruct((length, width), F32),
        ),
        in_specs=[vmem()] * len(args),
        out_specs=(vmem(),) * 4,
        scratch_shapes=[pltpu.VMEM((length, HEAD_DIM), BF)],
        input_output_aliases={} if first else {5: 3},
        compiler_params=pltpu.CompilerParams(vmem_limit_bytes=VMEM_LIMIT),
        name="attend_forward",
    )(*args)


def attend_backward_kernel(first, heads, block, *refs):
    if first:
        x, ag, wqkv, wout, qkv, mixed, lse, cos, sin, grads, total, dout, keys, vals, qn, dn, dqt, pg = refs
    else:
        x, ag, wqkv, wout, qkv, mixed, lse, cos, sin, carried, grads, total, dout, keys, vals, qn, dn, dqt, pg = refs
    hd = HEAD_DIM
    length = x.shape[0]
    scale = hd**-0.5
    dout[...] = nt(wout[: heads * hd, :], ag[...]).astype(BF)
    grads[3 * heads * hd :, :] = nn(mixed[...], ag[...])

    def one_head(h, _):
        base = pl.multiple_of(h * 3 * hd, 3 * hd)
        row = pl.multiple_of(h * hd, hd)
        c, s = cos[...], sin[...]
        keys[...] = qkv[pl.ds(base + hd, hd), :].T
        vals[...] = qkv[pl.ds(base + 2 * hd, hd), :].T
        qn[...] = qkv[pl.ds(base, hd), :].T
        dn[...] = dout[pl.ds(row, hd), :].T
        dk = jnp.zeros((length, hd), F32)
        dv = jnp.zeros((length, hd), F32)
        for b in range(length // block):
            cols = slice(b * block, (b + 1) * block)
            scores = nn(keys[...], qkv[pl.ds(base, hd), cols])
            probs = jnp.exp(scores - lse[pl.ds(pl.multiple_of(h * 8, 8), 1), cols])
            pgrad = nn(vals[...], dout[pl.ds(row, hd), cols])
            inner = jnp.sum(probs * pgrad, axis=0, keepdims=True)
            sgrad = (probs * (pgrad - inner)).astype(BF)
            dqt[:, cols] = nn(qkv[pl.ds(base + hd, hd), :], sgrad) * scale
            dk = dk + nn(sgrad, qn[cols, :])
            dv = dv + nn(probs.astype(BF), dn[cols, :])
        pg[pl.ds(base, hd), :] = rotate_back(dqt[...], c, s).astype(BF)
        pg[pl.ds(base + hd, hd), :] = rotate_back(dk.T, c, s).astype(BF)
        pg[pl.ds(base + 2 * hd, hd), :] = dv.T.astype(BF)
        return 0

    lax.fori_loop(0, heads, one_head, 0)
    grads[: 3 * heads * hd, :] = nn(pg[...], x[...])
    part = tn(pg[...], wqkv[...])
    total[...] = part if first else carried[...] + part


def attend_backward(x, ag, wqkv, wout, qkv, mixed, lse, cos, sin, carried):
    length, width = x.shape
    heads = wqkv.shape[0] // (3 * HEAD_DIM)
    block = min(256, length)
    first = carried is None
    args = (x, ag, wqkv, wout, qkv, mixed, lse, cos, sin) + (() if first else (carried,))
    half = pltpu.VMEM((length, HEAD_DIM), BF)
    return pl.pallas_call(
        functools.partial(attend_backward_kernel, first, heads, block),
        out_shape=(
            jax.ShapeDtypeStruct((4 * heads * HEAD_DIM, width), F32),
            jax.ShapeDtypeStruct((length, width), F32),
        ),
        in_specs=[vmem()] * len(args),
        out_specs=(vmem(),) * 2,
        scratch_shapes=[
            pltpu.VMEM((heads * HEAD_DIM, length), BF),
            half,
            half,
            half,
            half,
            pltpu.VMEM((HEAD_DIM, length), F32),
            pltpu.VMEM((3 * heads * HEAD_DIM, length), BF),
        ],
        input_output_aliases={} if first else {9: 1},
        compiler_params=pltpu.CompilerParams(vmem_limit_bytes=VMEM_LIMIT),
        name="attend_backward",
    )(*args)


def feed_kernel(first, *refs):
    if first:
        x, fg, up, down, bias, grads, bias_grad, out, xg = refs
    else:
        x, fg, up, down, bias, out_in, xg_in, grads, bias_grad, out, xg = refs
    step = pl.program_id(0)
    root = math.sqrt(2.0 / math.pi)
    u = nn(x[...], up[...]) + bias[0:1, :].astype(F32)
    square = u * u
    t = jnp.tanh(root * (u + 0.044715 * (square * u)))
    cdf = 0.5 * (1.0 + t)
    hidden = (u * cdf).astype(BF)
    slope = cdf + 0.5 * u * (1.0 - t * t) * (root * (1.0 + 3.0 * 0.044715 * square))
    dh = (nt(fg[...], down[...]) * slope).astype(BF)
    bias_grad[...] = jnp.broadcast_to(
        jnp.sum(dh.astype(F32), axis=0, keepdims=True), bias_grad.shape
    )
    grads[0, :, :] = nn(dh.T, x[...])
    grads[1, :, :] = nn(hidden.T, fg[...])
    out_part = nn(hidden, down[...])
    xg_part = nt(dh, up[...])

    @pl.when(step == 0)
    def _():
        out[...] = out_part if first else out_in[...] + out_part
        xg[...] = xg_part if first else xg_in[...] + xg_part

    @pl.when(step > 0)
    def _():
        out[...] += out_part
        xg[...] += xg_part


def feed(x, fg, up, down, packed, bias_block, carried):
    length, width = x.shape
    units = up.shape[1]
    block = min(256, units)
    first = carried is None
    whole = pl.BlockSpec((length, width), lambda i: (0, 0))
    args = (x, fg, up, down, packed) + (() if first else tuple(carried))
    n = len(args)
    return pl.pallas_call(
        functools.partial(feed_kernel, first),
        grid=(units // block,),
        out_shape=(
            jax.ShapeDtypeStruct((2, units, width), F32),
            jax.ShapeDtypeStruct((8, units), F32),
            jax.ShapeDtypeStruct((length, width), F32),
            jax.ShapeDtypeStruct((length, width), F32),
        ),
        in_specs=[
            whole,
            whole,
            pl.BlockSpec((width, block), lambda i: (0, i)),
            pl.BlockSpec((block, width), lambda i: (i, 0)),
            pl.BlockSpec((16, block), lambda i: (bias_block, i)),
        ]
        + [whole] * (n - 5),
        out_specs=(
            pl.BlockSpec((2, block, width), lambda i: (0, i, 0)),
            pl.BlockSpec((8, block), lambda i: (0, i)),
            whole,
            whole,
        ),
        input_output_aliases={} if first else {5: 2, 6: 3},
        compiler_params=pltpu.CompilerParams(vmem_limit_bytes=VMEM_LIMIT),
        name="feed",
    )(*args)


def swap(value, axis, size, bit):
    return lax.ppermute(value, axis, [(d, d ^ bit) for d in range(size)])


def factors_of(size):
    found, stride = [], 1
    while stride < size:
        factor = 2 if stride == 1 or size // stride < 4 else 4
        found.append((factor, stride))
        stride *= factor
    return found


def chunk_of(value, index, count):
    rows = value.shape[0] // count
    return lax.dynamic_slice_in_dim(value, index * rows, rows, 0)


def scatter_over_groups(value, size):
    index = lax.axis_index("dp")
    for factor, stride in factors_of(size):
        mine = (index // stride) % factor
        arrived = [
            swap(chunk_of(value, mine ^ r, factor).astype(BF), "dp", size, r * stride)
            for r in range(1, factor)
        ]
        kept = chunk_of(value, mine, factor)
        for piece in arrived:
            kept = kept + piece.astype(F32)
        value = kept
    return value


def in_order(pieces, mine):
    bit = 1
    while bit < len(pieces):
        on = (mine & bit) > 0
        pieces = [jnp.where(on, pieces[k ^ bit], pieces[k]) for k in range(len(pieces))]
        bit *= 2
    return pieces


def gather_over_groups(piece, size):
    index = lax.axis_index("dp")
    for factor, stride in reversed(factors_of(size)):
        mine = (index // stride) % factor
        pieces = [piece] + [swap(piece, "dp", size, r * stride) for r in range(1, factor)]
        piece = jnp.concatenate(in_order(pieces, mine), axis=0)
    return piece


def reduce_quarters(parts, groups):
    own = parts[0] + swap(parts[1], "tensor", 4, 1)
    other = parts[2] + swap(parts[3], "tensor", 4, 1)
    own = own + swap(other.astype(BF), "tensor", 4, 2).astype(F32)
    return gather_over_groups(scatter_over_groups(own, groups).astype(BF), groups)


def everywhere(rows, sums, quarters, groups):
    stages = [("tensor", 4, 1), ("tensor", 4, 2)]
    stages += [("dp", groups, 1 << k) for k in range(groups.bit_length() - 1)]
    for axis, size, bit in stages:
        count, width = rows.shape
        flat = [rows.reshape(1, count * width), sums]
        if quarters is not None:
            if len(quarters) > 1:
                flat += quarters[1::2]
            else:
                flat += quarters
        came = swap(jnp.concatenate(flat, axis=1), axis, size, bit)
        rest = came[:, count * width :]
        came_rows = came[:, : count * width].reshape(count, width)
        on = (lax.axis_index(axis) & bit) > 0
        rows = jnp.concatenate(
            [jnp.where(on, came_rows, rows), jnp.where(on, rows, came_rows)], axis=0
        )
        if quarters is not None:
            keep = quarters[0::2]
            span = quarters[0].shape[1]
            tail = rest[:, sums.shape[1] :]
            quarters = [q + tail[:, k * span : (k + 1) * span] for k, q in enumerate(keep)]
        sums = sums + rest[:, : sums.shape[1]]
    return rows, sums, quarters


def normed(values):
    center = values - jnp.mean(values, axis=-1, keepdims=True)
    variance = jnp.mean(center * center, axis=-1, keepdims=True)
    inverse = lax.rsqrt(variance + EPS)
    return center * inverse, inverse


def norm_back(grad, n, inverse, gain, scale):
    u = grad * (1.0 + scale) * gain
    return inverse * (
        u - jnp.mean(u, axis=-1, keepdims=True) - n * jnp.mean(u * n, axis=-1, keepdims=True)
    )


def rotary(length):
    half = HEAD_DIM // 2
    frequency = jnp.exp(jnp.arange(half, dtype=F32) * (-2.0 * math.log(10000.0) / HEAD_DIM))
    angles = frequency[:, None] * jnp.arange(length, dtype=jnp.int32).astype(F32)[None, :]
    return jnp.cos(angles), jnp.sin(angles)


def exact(left, right, contract):
    return lax.dot_general(
        left,
        right,
        (contract, ((), ())),
        precision=lax.Precision.HIGHEST,
        preferred_element_type=F32,
    )


def per_device(
    groups,
    tokens,
    cotangent,
    span_start,
    span_length,
    timestep,
    cond_table,
    mask_embed,
    ada_weight,
    ada_bias,
    first_gain,
    qkv_weight,
    out_weight,
    second_gain,
    up_weight,
    up_bias,
    down_weight,
    down_bias,
):
    _, length, width = tokens.shape
    packed = jnp.concatenate(
        [out_weight, jnp.broadcast_to(up_bias[None, :], (16, up_bias.shape[0]))], axis=0
    )
    bias_block = out_weight.shape[0] // 16

    def quarters_of(own):
        across = swap(own, "tensor", 4, 2)
        return [own, swap(own, "tensor", 4, 1), across, swap(across, "tensor", 4, 1)]

    wqkv = quarters_of(qkv_weight.T)
    wout = quarters_of(packed)
    wup = quarters_of(up_weight)
    wdown = quarters_of(down_weight)

    cos, sin = rotary(length)
    raw = lax.dynamic_slice_in_dim(cond_table, timestep[0], 1, 0)
    sig = jax.nn.sigmoid(raw)
    condition = raw * sig
    modulation = jnp.sum(condition.T * ada_weight, axis=0, keepdims=True) + ada_bias[None, :]
    shift_one, scale_one, gate_one, shift_two, scale_two, gate_two = jnp.split(modulation, 6, axis=1)
    positions = jnp.arange(length, dtype=jnp.int32)[:, None]
    masked = (positions >= span_start[0]) & (positions < span_start[0] + span_length[0])
    start_rows = jnp.where(masked, mask_embed[None, :], tokens[0].astype(F32))
    n_one, inverse_one = normed(start_rows)
    first_low = (n_one * first_gain[None, :] * (1.0 + scale_one) + shift_one).astype(BF)

    attention_out = None
    kept = []
    for j in range(4):
        qkv, mixed, lse, attention_out = attend_forward(
            first_low, wqkv[j], wout[j], cos, sin, attention_out
        )
        kept.append((qkv, mixed, lse))

    middle = start_rows + gate_one * attention_out
    n_two, inverse_two = normed(middle)
    second_low = (n_two * second_gain[None, :] * (1.0 + scale_two) + shift_two).astype(BF)
    upstream = cotangent[0].astype(F32)
    feed_grad = (gate_two * upstream).astype(BF)

    carried = None
    feed_parts, bias_parts = [None] * 4, [None] * 4
    for j in (0, 1, 2, 3):
        part, bias_part, *carried = feed(
            second_low, feed_grad, wup[j], wdown[j], wout[j], bias_block, carried
        )
        feed_parts[j] = part.reshape(2 * part.shape[1], width)
        bias_parts[j] = bias_part[0:1]
    feed_sum, second_grad = carried
    feed_out = feed_sum + down_bias.astype(F32)[None, :]
    layer_out = (middle + gate_two * feed_out).astype(BF)
    gate_two_grad = jnp.sum(upstream * feed_out, axis=0, keepdims=True)
    down_bias_grad = jnp.sum(feed_grad.astype(F32), axis=0, keepdims=True)
    shift_two_grad = jnp.sum(second_grad, axis=0, keepdims=True)
    product_two = jnp.sum(second_grad * n_two, axis=0, keepdims=True)
    scale_two_grad = product_two * second_gain[None, :]
    second_gain_grad = product_two * (1.0 + scale_two)
    middle_grad = upstream + norm_back(
        second_grad, n_two, inverse_two, second_gain[None, :], scale_two
    )
    gate_one_grad = jnp.sum(middle_grad * attention_out, axis=0, keepdims=True)
    attention_grad = (gate_one * middle_grad).astype(BF)
    feed_final = reduce_quarters(feed_parts, groups).astype(F32)

    early_rows, early_sums, early_quarter = everywhere(
        jnp.concatenate(
            [
                gate_one_grad,
                shift_two_grad,
                scale_two_grad,
                gate_two_grad,
                condition,
                jnp.broadcast_to(timestep.astype(F32)[:, None], (1, 128)),
            ],
            axis=1,
        ),
        jnp.concatenate([second_gain_grad, down_bias_grad], axis=1),
        bias_parts,
        groups,
    )

    first_grad = None
    attention_parts = [None] * 4
    for j in (3, 2, 1, 0):
        attention_parts[j], first_grad = attend_backward(
            first_low, attention_grad, wqkv[j], wout[j], *kept[j], cos, sin, first_grad
        )
    attention_final = reduce_quarters(attention_parts, groups).astype(F32)

    shift_one_grad = jnp.sum(first_grad, axis=0, keepdims=True)
    product_one = jnp.sum(first_grad * n_one, axis=0, keepdims=True)
    scale_one_grad = product_one * first_gain[None, :]
    first_gain_grad = product_one * (1.0 + scale_one)
    start_grad = middle_grad + norm_back(
        first_grad, n_one, inverse_one, first_gain[None, :], scale_one
    )
    tokens_grad = jnp.where(masked, 0.0, start_grad)[None]
    mask_grad = jnp.sum(jnp.where(masked, start_grad, 0.0), axis=0, keepdims=True)

    own_modulation = jnp.concatenate(
        [shift_one_grad, scale_one_grad, gate_one_grad, shift_two_grad, scale_two_grad, gate_two_grad],
        axis=1,
    )
    cond_grad = jnp.sum(ada_weight * own_modulation, axis=1)[None, :]
    cond_grad = cond_grad * (sig * (1.0 + raw * (1.0 - sig)))
    late_rows, late_sums, _ = everywhere(
        jnp.concatenate([shift_one_grad, scale_one_grad, cond_grad], axis=1),
        jnp.concatenate([mask_grad, first_gain_grad], axis=1),
        None,
        groups,
    )

    conditions = early_rows[:, 4 * width : 4 * width + 128]
    steps = early_rows[:, 4 * width + 128 : 4 * width + 129].astype(jnp.int32)
    all_modulation = jnp.concatenate([late_rows[:, : 2 * width], early_rows[:, : 4 * width]], axis=1)
    ada_weight_grad = exact(conditions, all_modulation, ((0,), (0,)))
    ada_bias_grad = jnp.sum(all_modulation, axis=0)
    chosen = (steps == jnp.arange(cond_table.shape[0], dtype=jnp.int32)[None, :]).astype(F32)
    table_grad = exact(chosen, late_rows[:, 2 * width :], ((0,), (0,)))

    units = up_weight.shape[1]
    heads_rows = qkv_weight.shape[1]
    return (
        layer_out[None],
        tokens_grad,
        table_grad,
        late_sums[0, :width],
        ada_weight_grad,
        ada_bias_grad,
        late_sums[0, width:],
        attention_final[:heads_rows].T,
        attention_final[heads_rows:],
        early_sums[0, :width],
        feed_final[:units].T,
        early_quarter[0][0],
        feed_final[units:],
        early_sums[0, width:],
    )


def solution(mesh):
    rows = P(("dp", "tensor"), None, None)
    each = P(("dp", "tensor"))
    columns = P(None, "tensor")
    lines = P("tensor", None)
    return jax.shard_map(
        functools.partial(per_device, mesh.shape["dp"]),
        mesh=mesh,
        in_specs=(
            rows, rows, each, each, each, P(), P(), P(), P(), P(),
            columns, lines, P(), columns, P("tensor"), lines, P(),
        ),
        out_specs=(
            rows, rows, P(), P(), P(), P(), P(), columns, lines, P(),
            columns, P("tensor"), lines, P(),
        ),
        check_vma=False,
    )
```

```python
import functools
import math

import jax
import jax.numpy as jnp
from jax import lax
from jax.experimental import pallas as pl
from jax.experimental.pallas import tpu as pltpu
from jax.sharding import PartitionSpec as P


HEAD_DIM = 64
BF = jnp.bfloat16
F32 = jnp.float32
EPS = 1e-05
VMEM_LIMIT = 58 * 1024 * 1024


def nn(left, right):
    return lax.dot_general(left, right, (((1,), (0,)), ((), ())), preferred_element_type=F32)


def nt(left, right):
    return lax.dot_general(left, right, (((1,), (1,)), ((), ())), preferred_element_type=F32)


def tn(left, right):
    return lax.dot_general(left, right, (((0,), (0,)), ((), ())), preferred_element_type=F32)


def vmem():
    return pl.BlockSpec(memory_space=pltpu.VMEM)


def rotate(u, c, s):
    half = u.shape[0] // 2
    a, b = u[:half], u[half:]
    return jnp.concatenate([a * c - b * s, b * c + a * s], axis=0)


def rotate_back(w, c, s):
    half = w.shape[0] // 2
    a, b = w[:half], w[half:]
    return jnp.concatenate([a * c + b * s, b * c - a * s], axis=0)


def attend_forward_kernel(first, heads, block, *refs):
    if first:
        x, wqkv, wout, cos, sin, qkv, mixed, lse, total, keys = refs
    else:
        x, wqkv, wout, cos, sin, carried, qkv, mixed, lse, total, keys = refs
    hd = HEAD_DIM
    length = x.shape[0]

    def one_head(h, _):
        base = pl.multiple_of(h * 3 * hd, 3 * hd)
        projected = nt(wqkv[pl.ds(base, 3 * hd), :], x[...])
        c, s = cos[...], sin[...]
        qkv[pl.ds(base, hd), :] = rotate(projected[:hd], c, s).astype(BF) * BF(hd**-0.5)
        key = rotate(projected[hd : 2 * hd], c, s).astype(BF)
        qkv[pl.ds(base + hd, hd), :] = key
        qkv[pl.ds(base + 2 * hd, hd), :] = projected[2 * hd :].astype(BF)
        keys[...] = key.T
        for b in range(length // block):
            cols = slice(b * block, (b + 1) * block)
            scores = nn(keys[...], qkv[pl.ds(base, hd), cols])
            top = jnp.max(scores, axis=0, keepdims=True)
            power = jnp.exp(scores - top)
            norm = jnp.sum(power, axis=0, keepdims=True)
            probs = (power * (1.0 / norm)).astype(BF)
            out = nn(qkv[pl.ds(base + 2 * hd, hd), :], probs)
            mixed[pl.ds(pl.multiple_of(h * hd, hd), hd), cols] = out.astype(BF)
            lse[pl.ds(pl.multiple_of(h * 8, 8), 8), cols] = jnp.broadcast_to(
                top + jnp.log(norm), (8, block)
            )
        return 0

    lax.fori_loop(0, heads, one_head, 0)
    part = tn(mixed[...], wout[: heads * hd, :])
    total[...] = part if first else carried[...] + part


def attend_forward(x, wqkv, wout, cos, sin, carried):
    length, width = x.shape
    heads = wqkv.shape[0] // (3 * HEAD_DIM)
    block = min(256, length)
    first = carried is None
    args = (x, wqkv, wout, cos, sin) + (() if first else (carried,))
    return pl.pallas_call(
        functools.partial(attend_forward_kernel, first, heads, block),
        out_shape=(
            jax.ShapeDtypeStruct((3 * heads * HEAD_DIM, length), BF),
            jax.ShapeDtypeStruct((heads * HEAD_DIM, length), BF),
            jax.ShapeDtypeStruct((heads * 8, length), F32),
            jax.ShapeDtypeStruct((length, width), F32),
        ),
        in_specs=[vmem()] * len(args),
        out_specs=(vmem(),) * 4,
        scratch_shapes=[pltpu.VMEM((length, HEAD_DIM), BF)],
        input_output_aliases={} if first else {5: 3},
        compiler_params=pltpu.CompilerParams(vmem_limit_bytes=VMEM_LIMIT),
        name="attend_forward",
    )(*args)


def attend_backward_kernel(first, heads, block, *refs):
    if first:
        x, ag, wqkv, wout, qkv, mixed, lse, cos, sin, grads, total, dout, keys, vals, qn, dn, dqt, pg = refs
    else:
        x, ag, wqkv, wout, qkv, mixed, lse, cos, sin, carried, grads, total, dout, keys, vals, qn, dn, dqt, pg = refs
    hd = HEAD_DIM
    length = x.shape[0]
    scale = hd**-0.5
    dout[...] = nt(wout[: heads * hd, :], ag[...]).astype(BF)
    grads[3 * heads * hd :, :] = nn(mixed[...], ag[...])

    def one_head(h, _):
        base = pl.multiple_of(h * 3 * hd, 3 * hd)
        row = pl.multiple_of(h * hd, hd)
        c, s = cos[...], sin[...]
        keys[...] = qkv[pl.ds(base + hd, hd), :].T
        vals[...] = qkv[pl.ds(base + 2 * hd, hd), :].T
        qn[...] = qkv[pl.ds(base, hd), :].T
        dn[...] = dout[pl.ds(row, hd), :].T
        dk = jnp.zeros((length, hd), F32)
        dv = jnp.zeros((length, hd), F32)
        for b in range(length // block):
            cols = slice(b * block, (b + 1) * block)
            scores = nn(keys[...], qkv[pl.ds(base, hd), cols])
            probs = jnp.exp(scores - lse[pl.ds(pl.multiple_of(h * 8, 8), 1), cols])
            pgrad = nn(vals[...], dout[pl.ds(row, hd), cols])
            inner = jnp.sum(probs * pgrad, axis=0, keepdims=True)
            sgrad = (probs * (pgrad - inner)).astype(BF)
            dqt[:, cols] = nn(qkv[pl.ds(base + hd, hd), :], sgrad) * scale
            dk = dk + nn(sgrad, qn[cols, :])
            dv = dv + nn(probs.astype(BF), dn[cols, :])
        pg[pl.ds(base, hd), :] = rotate_back(dqt[...], c, s).astype(BF)
        pg[pl.ds(base + hd, hd), :] = rotate_back(dk.T, c, s).astype(BF)
        pg[pl.ds(base + 2 * hd, hd), :] = dv.T.astype(BF)
        return 0

    lax.fori_loop(0, heads, one_head, 0)
    grads[: 3 * heads * hd, :] = nn(pg[...], x[...])
    part = tn(pg[...], wqkv[...])
    total[...] = part if first else carried[...] + part


def attend_backward(x, ag, wqkv, wout, qkv, mixed, lse, cos, sin, carried):
    length, width = x.shape
    heads = wqkv.shape[0] // (3 * HEAD_DIM)
    block = min(256, length)
    first = carried is None
    args = (x, ag, wqkv, wout, qkv, mixed, lse, cos, sin) + (() if first else (carried,))
    half = pltpu.VMEM((length, HEAD_DIM), BF)
    return pl.pallas_call(
        functools.partial(attend_backward_kernel, first, heads, block),
        out_shape=(
            jax.ShapeDtypeStruct((4 * heads * HEAD_DIM, width), F32),
            jax.ShapeDtypeStruct((length, width), F32),
        ),
        in_specs=[vmem()] * len(args),
        out_specs=(vmem(),) * 2,
        scratch_shapes=[
            pltpu.VMEM((heads * HEAD_DIM, length), BF),
            half,
            half,
            half,
            half,
            pltpu.VMEM((HEAD_DIM, length), F32),
            pltpu.VMEM((3 * heads * HEAD_DIM, length), BF),
        ],
        input_output_aliases={} if first else {9: 1},
        compiler_params=pltpu.CompilerParams(vmem_limit_bytes=VMEM_LIMIT),
        name="attend_backward",
    )(*args)


def feed_kernel(first, *refs):
    if first:
        x, fg, up, down, bias, grads, bias_grad, out, xg = refs
    else:
        x, fg, up, down, bias, out_in, xg_in, grads, bias_grad, out, xg = refs
    step = pl.program_id(0)
    root = math.sqrt(2.0 / math.pi)
    u = nn(x[...], up[...]) + bias[0:1, :].astype(F32)
    square = u * u
    t = jnp.tanh(root * (u + 0.044715 * (square * u)))
    cdf = 0.5 * (1.0 + t)
    hidden = (u * cdf).astype(BF)
    slope = cdf + 0.5 * u * (1.0 - t * t) * (root * (1.0 + 3.0 * 0.044715 * square))
    dh = (nt(fg[...], down[...]) * slope).astype(BF)
    bias_grad[...] = jnp.broadcast_to(
        jnp.sum(dh.astype(F32), axis=0, keepdims=True), bias_grad.shape
    )
    grads[0, :, :] = nn(dh.T, x[...])
    grads[1, :, :] = nn(hidden.T, fg[...])
    out_part = nn(hidden, down[...])
    xg_part = nt(dh, up[...])

    @pl.when(step == 0)
    def _():
        out[...] = out_part if first else out_in[...] + out_part
        xg[...] = xg_part if first else xg_in[...] + xg_part

    @pl.when(step > 0)
    def _():
        out[...] += out_part
        xg[...] += xg_part


def feed(x, fg, up, down, packed, bias_block, carried):
    length, width = x.shape
    units = up.shape[1]
    block = min(256, units)
    first = carried is None
    whole = pl.BlockSpec((length, width), lambda i: (0, 0))
    args = (x, fg, up, down, packed) + (() if first else tuple(carried))
    n = len(args)
    return pl.pallas_call(
        functools.partial(feed_kernel, first),
        grid=(units // block,),
        out_shape=(
            jax.ShapeDtypeStruct((2, units, width), F32),
            jax.ShapeDtypeStruct((8, units), F32),
            jax.ShapeDtypeStruct((length, width), F32),
            jax.ShapeDtypeStruct((length, width), F32),
        ),
        in_specs=[
            whole,
            whole,
            pl.BlockSpec((width, block), lambda i: (0, i)),
            pl.BlockSpec((block, width), lambda i: (i, 0)),
            pl.BlockSpec((16, block), lambda i: (bias_block, i)),
        ]
        + [whole] * (n - 5),
        out_specs=(
            pl.BlockSpec((2, block, width), lambda i: (0, i, 0)),
            pl.BlockSpec((8, block), lambda i: (0, i)),
            whole,
            whole,
        ),
        input_output_aliases={} if first else {5: 2, 6: 3},
        compiler_params=pltpu.CompilerParams(vmem_limit_bytes=VMEM_LIMIT),
        name="feed",
    )(*args)


def swap(value, axis, size, bit):
    return lax.ppermute(value, axis, [(d, d ^ bit) for d in range(size)])


def factors_of(size):
    found, stride = [], 1
    while stride < size:
        factor = 2 if stride == 1 or size // stride < 4 else 4
        found.append((factor, stride))
        stride *= factor
    return found


def chunk_of(value, index, count):
    rows = value.shape[0] // count
    return lax.dynamic_slice_in_dim(value, index * rows, rows, 0)


def scatter_stages(value, size):
    index = lax.axis_index("dp")
    for factor, stride in factors_of(size):
        mine = (index // stride) % factor
        sent = [chunk_of(value, mine ^ r, factor).astype(BF) for r in range(1, factor)]
        kept = chunk_of(value, mine, factor)
        sent, kept = yield sent, kept
        arrived = [swap(s, "dp", size, (r + 1) * stride) for r, s in enumerate(sent)]
        for piece in arrived:
            kept = kept + piece.astype(F32)
        value = kept
    piece = value.astype(BF)
    for factor, stride in reversed(factors_of(size)):
        mine = (index // stride) % factor
        sent, _ = yield [piece], None
        piece = sent[0]
        pieces = [piece] + [swap(piece, "dp", size, r * stride) for r in range(1, factor)]
        piece = jnp.concatenate(in_order(pieces, mine), axis=0)
    yield None, piece


class Chain:
    def __init__(self, value, size):
        self.steps = scatter_stages(value, size)
        self.sent, self.kept = next(self.steps)

    def tie(self, token):
        if self.sent is None:
            return token
        if self.kept is None:
            token, self.sent = lax.optimization_barrier((token, self.sent))
        else:
            token, self.sent, self.kept = lax.optimization_barrier((token, self.sent, self.kept))
        return token

    def advance(self):
        if self.sent is not None:
            self.sent, self.kept = self.steps.send((self.sent, self.kept))

    def finish(self):
        while self.sent is not None:
            self.advance()
        return self.kept


def in_order(pieces, mine):
    bit = 1
    while bit < len(pieces):
        on = (mine & bit) > 0
        pieces = [jnp.where(on, pieces[k ^ bit], pieces[k]) for k in range(len(pieces))]
        bit *= 2
    return pieces


class Flow:
    def __init__(self, rows, sums, quarters, groups):
        self.rows, self.sums, self.quarters = rows, sums, quarters
        self.stages = [("tensor", 4, 1), ("tensor", 4, 2)]
        self.stages += [("dp", groups, 1 << k) for k in range(groups.bit_length() - 1)]

    def tie(self, token):
        token, self.rows, self.sums = lax.optimization_barrier((token, self.rows, self.sums))
        return token

    def advance(self):
        if not self.stages:
            return
        axis, size, bit = self.stages.pop(0)
        rows, sums, quarters = self.rows, self.sums, self.quarters
        count, width = rows.shape
        flat = [rows.reshape(1, count * width), sums]
        if quarters is not None:
            flat += quarters[1::2] if len(quarters) > 1 else quarters
        came = swap(jnp.concatenate(flat, axis=1), axis, size, bit)
        rest = came[:, count * width :]
        came_rows = came[:, : count * width].reshape(count, width)
        on = (lax.axis_index(axis) & bit) > 0
        self.rows = jnp.concatenate(
            [jnp.where(on, came_rows, rows), jnp.where(on, rows, came_rows)], axis=0
        )
        if quarters is not None:
            span = quarters[0].shape[1]
            tail = rest[:, sums.shape[1] :]
            self.quarters = [
                q + tail[:, k * span : (k + 1) * span] for k, q in enumerate(quarters[0::2])
            ]
        self.sums = sums + rest[:, : sums.shape[1]]

    def finish(self):
        while self.stages:
            self.advance()
        return self.rows, self.sums, self.quarters


def tie(token, value):
    return lax.optimization_barrier((token, value))


def normed(values):
    center = values - jnp.mean(values, axis=-1, keepdims=True)
    variance = jnp.mean(center * center, axis=-1, keepdims=True)
    inverse = lax.rsqrt(variance + EPS)
    return center * inverse, inverse


def norm_back(grad, n, inverse, gain, scale):
    u = grad * (1.0 + scale) * gain
    return inverse * (
        u - jnp.mean(u, axis=-1, keepdims=True) - n * jnp.mean(u * n, axis=-1, keepdims=True)
    )


def rotary(length):
    half = HEAD_DIM // 2
    frequency = jnp.exp(jnp.arange(half, dtype=F32) * (-2.0 * math.log(10000.0) / HEAD_DIM))
    angles = frequency[:, None] * jnp.arange(length, dtype=jnp.int32).astype(F32)[None, :]
    return jnp.cos(angles), jnp.sin(angles)


def exact(left, right, contract):
    return lax.dot_general(
        left,
        right,
        (contract, ((), ())),
        precision=lax.Precision.HIGHEST,
        preferred_element_type=F32,
    )


def per_device(
    groups,
    tokens,
    cotangent,
    span_start,
    span_length,
    timestep,
    cond_table,
    mask_embed,
    ada_weight,
    ada_bias,
    first_gain,
    qkv_weight,
    out_weight,
    second_gain,
    up_weight,
    up_bias,
    down_weight,
    down_bias,
):
    _, length, width = tokens.shape
    packed = jnp.concatenate(
        [out_weight, jnp.broadcast_to(up_bias[None, :], (16, up_bias.shape[0]))], axis=0
    )
    bias_block = out_weight.shape[0] // 16

    own_qkv = qkv_weight.T
    wqkv = [own_qkv, swap(own_qkv, "tensor", 4, 1), swap(own_qkv, "tensor", 4, 2), None]
    wout = [packed, swap(packed, "tensor", 4, 1), swap(packed, "tensor", 4, 2), None]
    wup = [up_weight, swap(up_weight, "tensor", 4, 1), None, None]
    wdown = [down_weight, swap(down_weight, "tensor", 4, 1), None, None]

    cos, sin = rotary(length)
    raw = lax.dynamic_slice_in_dim(cond_table, timestep[0], 1, 0)
    sig = jax.nn.sigmoid(raw)
    condition = raw * sig
    modulation = jnp.sum(condition.T * ada_weight, axis=0, keepdims=True) + ada_bias[None, :]
    shift_one, scale_one, gate_one, shift_two, scale_two, gate_two = jnp.split(modulation, 6, axis=1)
    positions = jnp.arange(length, dtype=jnp.int32)[:, None]
    masked = (positions >= span_start[0]) & (positions < span_start[0] + span_length[0])
    start_rows = jnp.where(masked, mask_embed[None, :], tokens[0].astype(F32))
    n_one, inverse_one = normed(start_rows)
    first_low = (n_one * first_gain[None, :] * (1.0 + scale_one) + shift_one).astype(BF)

    attention_out = None
    kept = []
    for j in range(4):
        qkv, mixed, lse, attention_out = attend_forward(
            first_low, wqkv[j], wout[j], cos, sin, attention_out
        )
        if j == 0:
            lse, (wqkv[2], wout[2], up_weight) = tie(lse, (wqkv[2], wout[2], up_weight))
            wqkv[3] = swap(wqkv[2], "tensor", 4, 1)
            wout[3] = swap(wout[2], "tensor", 4, 1)
            wup[2] = swap(up_weight, "tensor", 4, 2)
        if j == 1:
            lse, down_weight = tie(lse, down_weight)
            wdown[2] = swap(down_weight, "tensor", 4, 2)
        if j == 3:
            lse, wup[2] = tie(lse, wup[2])
            wup[3] = swap(wup[2], "tensor", 4, 1)
        kept.append((qkv, mixed, lse))

    middle = start_rows + gate_one * attention_out
    n_two, inverse_two = normed(middle)
    second_low = (n_two * second_gain[None, :] * (1.0 + scale_two) + shift_two).astype(BF)
    upstream = cotangent[0].astype(F32)
    feed_grad = (gate_two * upstream).astype(BF)

    carried = None
    feed_parts, bias_parts = [None] * 4, [None] * 4
    for j in (0, 3, 2, 1):
        part, bias_part, *carried = feed(
            second_low, feed_grad, wup[j], wdown[j], wout[j], bias_block, carried
        )
        feed_parts[j] = part.reshape(2 * part.shape[1], width)
        bias_parts[j] = bias_part[0:1]
        if j == 0:
            bias_parts[0], wdown[2] = tie(bias_parts[0], wdown[2])
            wdown[3] = swap(wdown[2], "tensor", 4, 1)
        if j == 2:
            feed_other = (feed_parts[2] + swap(feed_parts[3], "tensor", 4, 1)).astype(BF)
            wup[1], feed_other = tie(wup[1], feed_other)
            feed_across = swap(feed_other, "tensor", 4, 2)
    feed_sum, second_grad = carried
    feed_out = feed_sum + down_bias.astype(F32)[None, :]
    layer_out = (middle + gate_two * feed_out).astype(BF)
    gate_two_grad = jnp.sum(upstream * feed_out, axis=0, keepdims=True)
    down_bias_grad = jnp.sum(feed_grad.astype(F32), axis=0, keepdims=True)
    shift_two_grad = jnp.sum(second_grad, axis=0, keepdims=True)
    product_two = jnp.sum(second_grad * n_two, axis=0, keepdims=True)
    scale_two_grad = product_two * second_gain[None, :]
    second_gain_grad = product_two * (1.0 + scale_two)
    middle_grad = upstream + norm_back(
        second_grad, n_two, inverse_two, second_gain[None, :], scale_two
    )
    gate_one_grad = jnp.sum(middle_grad * attention_out, axis=0, keepdims=True)
    attention_grad = (gate_one * middle_grad).astype(BF)
    early = Flow(
        jnp.concatenate(
            [
                gate_one_grad,
                shift_two_grad,
                scale_two_grad,
                gate_two_grad,
                condition,
                jnp.broadcast_to(timestep.astype(F32)[:, None], (1, 128)),
            ],
            axis=1,
        ),
        jnp.concatenate([second_gain_grad, down_bias_grad], axis=1),
        bias_parts,
        groups,
    )

    first_grad = None
    parts = [None] * 4
    lses = {j: kept[j][2] for j in range(4)}
    for j in (3, 2, 1, 0):
        parts[j], first_grad = attend_backward(
            first_low, attention_grad, wqkv[j], wout[j], *kept[j][:2], lses[j], cos, sin, first_grad
        )
        first_grad, parts[j] = tie(first_grad, parts[j])
        if j == 3:
            feed_chain = Chain(
                feed_parts[0] + swap(feed_parts[1], "tensor", 4, 1) + feed_across.astype(F32), groups
            )
        else:
            feed_chain.advance()
        early.advance()
        if j == 2:
            other = (parts[2] + swap(parts[3], "tensor", 4, 1)).astype(BF)
            lses[1], other = tie(lses[1], other)
            across = swap(other, "tensor", 4, 2)
        if j > 0:
            lses[j - 1] = early.tie(feed_chain.tie(lses[j - 1]))
    chain = Chain(parts[0] + swap(parts[1], "tensor", 4, 1) + across.astype(F32), groups)
    feed_final = feed_chain.finish().astype(F32)
    attention_final = chain.finish().astype(F32)
    early_rows, early_sums, early_quarter = early.finish()

    shift_one_grad = jnp.sum(first_grad, axis=0, keepdims=True)
    product_one = jnp.sum(first_grad * n_one, axis=0, keepdims=True)
    scale_one_grad = product_one * first_gain[None, :]
    first_gain_grad = product_one * (1.0 + scale_one)
    start_grad = middle_grad + norm_back(
        first_grad, n_one, inverse_one, first_gain[None, :], scale_one
    )
    tokens_grad = jnp.where(masked, 0.0, start_grad)[None]
    mask_grad = jnp.sum(jnp.where(masked, start_grad, 0.0), axis=0, keepdims=True)

    own_modulation = jnp.concatenate(
        [shift_one_grad, scale_one_grad, gate_one_grad, shift_two_grad, scale_two_grad, gate_two_grad],
        axis=1,
    )
    cond_grad = jnp.sum(ada_weight * own_modulation, axis=1)[None, :]
    cond_grad = cond_grad * (sig * (1.0 + raw * (1.0 - sig)))
    late_rows, late_sums, _ = Flow(
        jnp.concatenate([shift_one_grad, scale_one_grad, cond_grad], axis=1),
        jnp.concatenate([mask_grad, first_gain_grad], axis=1),
        None,
        groups,
    ).finish()

    conditions = early_rows[:, 4 * width : 4 * width + 128]
    steps = early_rows[:, 4 * width + 128 : 4 * width + 129].astype(jnp.int32)
    all_modulation = jnp.concatenate([late_rows[:, : 2 * width], early_rows[:, : 4 * width]], axis=1)
    ada_weight_grad = exact(conditions, all_modulation, ((0,), (0,)))
    ada_bias_grad = jnp.sum(all_modulation, axis=0)
    chosen = (steps == jnp.arange(cond_table.shape[0], dtype=jnp.int32)[None, :]).astype(F32)
    table_grad = exact(chosen, late_rows[:, 2 * width :], ((0,), (0,)))

    units = up_weight.shape[1]
    heads_rows = qkv_weight.shape[1]
    return (
        layer_out[None],
        tokens_grad,
        table_grad,
        late_sums[0, :width],
        ada_weight_grad,
        ada_bias_grad,
        late_sums[0, width:],
        attention_final[:heads_rows].T,
        attention_final[heads_rows:],
        early_sums[0, :width],
        feed_final[:units].T,
        early_quarter[0][0],
        feed_final[units:],
        early_sums[0, width:],
    )


def solution(mesh):
    rows = P(("dp", "tensor"), None, None)
    each = P(("dp", "tensor"))
    columns = P(None, "tensor")
    lines = P("tensor", None)

    def body(*arrays):
        return per_device(mesh.shape["dp"], *arrays)

    return jax.shard_map(
        body,
        mesh=mesh,
        in_specs=(
            rows, rows, each, each, each, P(), P(), P(), P(), P(),
            columns, lines, P(), columns, P("tensor"), lines, P(),
        ),
        out_specs=(
            rows, rows, P(), P(), P(), P(), P(), columns, lines, P(),
            columns, P("tensor"), lines, P(),
        ),
        check_vma=False,
    )
```

```python
import functools
import math

import jax
import jax.numpy as jnp
from jax import lax
from jax.experimental import pallas as pl
from jax.experimental.pallas import tpu as pltpu
from jax.sharding import PartitionSpec as P


HEAD_DIM = 64
BF = jnp.bfloat16
F32 = jnp.float32
EPS = 1e-05
VMEM_LIMIT = 58 * 1024 * 1024


def nn(left, right):
    return lax.dot_general(left, right, (((1,), (0,)), ((), ())), preferred_element_type=F32)


def nt(left, right):
    return lax.dot_general(left, right, (((1,), (1,)), ((), ())), preferred_element_type=F32)


def tn(left, right):
    return lax.dot_general(left, right, (((0,), (0,)), ((), ())), preferred_element_type=F32)


def vmem():
    return pl.BlockSpec(memory_space=pltpu.VMEM)


def rotate(u, c, s):
    half = u.shape[0] // 2
    a, b = u[:half], u[half:]
    return jnp.concatenate([a * c - b * s, b * c + a * s], axis=0)


def rotate_back(w, c, s):
    half = w.shape[0] // 2
    a, b = w[:half], w[half:]
    return jnp.concatenate([a * c + b * s, b * c - a * s], axis=0)


def attend_forward_kernel(first, heads, block, *refs):
    if first:
        x, wqkv, wout, cos, sin, qkv, mixed, lse, total, keys = refs
    else:
        x, wqkv, wout, cos, sin, carried, qkv, mixed, lse, total, keys = refs
    hd = HEAD_DIM
    length = x.shape[0]

    def one_head(h, _):
        base = pl.multiple_of(h * 3 * hd, 3 * hd)
        projected = nt(wqkv[pl.ds(base, 3 * hd), :], x[...])
        c, s = cos[...], sin[...]
        qkv[pl.ds(base, hd), :] = rotate(projected[:hd], c, s).astype(BF) * BF(hd**-0.5)
        key = rotate(projected[hd : 2 * hd], c, s).astype(BF)
        qkv[pl.ds(base + hd, hd), :] = key
        qkv[pl.ds(base + 2 * hd, hd), :] = projected[2 * hd :].astype(BF)
        keys[...] = key.T
        for b in range(length // block):
            cols = slice(b * block, (b + 1) * block)
            scores = nn(keys[...], qkv[pl.ds(base, hd), cols])
            top = jnp.max(scores, axis=0, keepdims=True)
            power = jnp.exp(scores - top)
            norm = jnp.sum(power, axis=0, keepdims=True)
            probs = (power * (1.0 / norm)).astype(BF)
            out = nn(qkv[pl.ds(base + 2 * hd, hd), :], probs)
            mixed[pl.ds(pl.multiple_of(h * hd, hd), hd), cols] = out.astype(BF)
            lse[pl.ds(pl.multiple_of(h * 8, 8), 8), cols] = jnp.broadcast_to(
                top + jnp.log(norm), (8, block)
            )
        return 0

    lax.fori_loop(0, heads, one_head, 0)
    part = tn(mixed[...], wout[: heads * hd, :])
    total[...] = part if first else carried[...] + part


def attend_forward(x, wqkv, wout, cos, sin, carried):
    length, width = x.shape
    heads = wqkv.shape[0] // (3 * HEAD_DIM)
    block = min(256, length)
    first = carried is None
    args = (x, wqkv, wout, cos, sin) + (() if first else (carried,))
    return pl.pallas_call(
        functools.partial(attend_forward_kernel, first, heads, block),
        out_shape=(
            jax.ShapeDtypeStruct((3 * heads * HEAD_DIM, length), BF),
            jax.ShapeDtypeStruct((heads * HEAD_DIM, length), BF),
            jax.ShapeDtypeStruct((heads * 8, length), F32),
            jax.ShapeDtypeStruct((length, width), F32),
        ),
        in_specs=[vmem()] * len(args),
        out_specs=(vmem(),) * 4,
        scratch_shapes=[pltpu.VMEM((length, HEAD_DIM), BF)],
        input_output_aliases={} if first else {5: 3},
        compiler_params=pltpu.CompilerParams(vmem_limit_bytes=VMEM_LIMIT),
        name="attend_forward",
    )(*args)


def attend_backward_kernel(first, heads, block, *refs):
    if first:
        x, ag, wqkv, wout, qkv, mixed, lse, cos, sin, grads, total, dout, keys, vals, qn, dn, dqt, pg = refs
    else:
        x, ag, wqkv, wout, qkv, mixed, lse, cos, sin, carried, grads, total, dout, keys, vals, qn, dn, dqt, pg = refs
    hd = HEAD_DIM
    length = x.shape[0]
    scale = hd**-0.5
    dout[...] = nt(wout[: heads * hd, :], ag[...]).astype(BF)
    grads[3 * heads * hd :, :] = nn(mixed[...], ag[...])

    def one_head(h, _):
        base = pl.multiple_of(h * 3 * hd, 3 * hd)
        row = pl.multiple_of(h * hd, hd)
        c, s = cos[...], sin[...]
        keys[...] = qkv[pl.ds(base + hd, hd), :].T
        vals[...] = qkv[pl.ds(base + 2 * hd, hd), :].T
        qn[...] = qkv[pl.ds(base, hd), :].T
        dn[...] = dout[pl.ds(row, hd), :].T
        dk = jnp.zeros((length, hd), F32)
        dv = jnp.zeros((length, hd), F32)
        for b in range(length // block):
            cols = slice(b * block, (b + 1) * block)
            scores = nn(keys[...], qkv[pl.ds(base, hd), cols])
            probs = jnp.exp(scores - lse[pl.ds(pl.multiple_of(h * 8, 8), 1), cols])
            pgrad = nn(vals[...], dout[pl.ds(row, hd), cols])
            inner = jnp.sum(probs * pgrad, axis=0, keepdims=True)
            sgrad = (probs * (pgrad - inner)).astype(BF)
            dqt[:, cols] = nn(qkv[pl.ds(base + hd, hd), :], sgrad) * scale
            dk = dk + nn(sgrad, qn[cols, :])
            dv = dv + nn(probs.astype(BF), dn[cols, :])
        pg[pl.ds(base, hd), :] = rotate_back(dqt[...], c, s).astype(BF)
        pg[pl.ds(base + hd, hd), :] = rotate_back(dk.T, c, s).astype(BF)
        pg[pl.ds(base + 2 * hd, hd), :] = dv.T.astype(BF)
        return 0

    lax.fori_loop(0, heads, one_head, 0)
    grads[: 3 * heads * hd, :] = nn(pg[...], x[...])
    part = tn(pg[...], wqkv[...])
    total[...] = part if first else carried[...] + part


def attend_backward(x, ag, wqkv, wout, qkv, mixed, lse, cos, sin, carried):
    length, width = x.shape
    heads = wqkv.shape[0] // (3 * HEAD_DIM)
    block = min(256, length)
    first = carried is None
    args = (x, ag, wqkv, wout, qkv, mixed, lse, cos, sin) + (() if first else (carried,))
    half = pltpu.VMEM((length, HEAD_DIM), BF)
    return pl.pallas_call(
        functools.partial(attend_backward_kernel, first, heads, block),
        out_shape=(
            jax.ShapeDtypeStruct((4 * heads * HEAD_DIM, width), F32),
            jax.ShapeDtypeStruct((length, width), F32),
        ),
        in_specs=[vmem()] * len(args),
        out_specs=(vmem(),) * 2,
        scratch_shapes=[
            pltpu.VMEM((heads * HEAD_DIM, length), BF),
            half,
            half,
            half,
            half,
            pltpu.VMEM((HEAD_DIM, length), F32),
            pltpu.VMEM((3 * heads * HEAD_DIM, length), BF),
        ],
        input_output_aliases={} if first else {9: 1},
        compiler_params=pltpu.CompilerParams(vmem_limit_bytes=VMEM_LIMIT),
        name="attend_backward",
    )(*args)


def feed_kernel(first, *refs):
    if first:
        x, fg, up, down, bias, grads, bias_grad, out, xg = refs
    else:
        x, fg, up, down, bias, out_in, xg_in, grads, bias_grad, out, xg = refs
    step = pl.program_id(0)
    root = math.sqrt(2.0 / math.pi)
    u = nn(x[...], up[...]) + bias[0:1, :].astype(F32)
    square = u * u
    t = jnp.tanh(root * (u + 0.044715 * (square * u)))
    cdf = 0.5 * (1.0 + t)
    hidden = (u * cdf).astype(BF)
    slope = cdf + 0.5 * u * (1.0 - t * t) * (root * (1.0 + 3.0 * 0.044715 * square))
    dh = (nt(fg[...], down[...]) * slope).astype(BF)
    bias_grad[...] = jnp.broadcast_to(
        jnp.sum(dh.astype(F32), axis=0, keepdims=True), bias_grad.shape
    )
    grads[0, :, :] = nn(dh.T, x[...])
    grads[1, :, :] = nn(hidden.T, fg[...])
    out_part = nn(hidden, down[...])
    xg_part = nt(dh, up[...])

    @pl.when(step == 0)
    def _():
        out[...] = out_part if first else out_in[...] + out_part
        xg[...] = xg_part if first else xg_in[...] + xg_part

    @pl.when(step > 0)
    def _():
        out[...] += out_part
        xg[...] += xg_part


def feed(x, fg, up, down, packed, bias_block, carried):
    length, width = x.shape
    units = up.shape[1]
    block = min(256, units)
    first = carried is None
    whole = pl.BlockSpec((length, width), lambda i: (0, 0))
    args = (x, fg, up, down, packed) + (() if first else tuple(carried))
    n = len(args)
    return pl.pallas_call(
        functools.partial(feed_kernel, first),
        grid=(units // block,),
        out_shape=(
            jax.ShapeDtypeStruct((2, units, width), F32),
            jax.ShapeDtypeStruct((8, units), F32),
            jax.ShapeDtypeStruct((length, width), F32),
            jax.ShapeDtypeStruct((length, width), F32),
        ),
        in_specs=[
            whole,
            whole,
            pl.BlockSpec((width, block), lambda i: (0, i)),
            pl.BlockSpec((block, width), lambda i: (i, 0)),
            pl.BlockSpec((16, block), lambda i: (bias_block, i)),
        ]
        + [whole] * (n - 5),
        out_specs=(
            pl.BlockSpec((2, block, width), lambda i: (0, i, 0)),
            pl.BlockSpec((8, block), lambda i: (0, i)),
            whole,
            whole,
        ),
        input_output_aliases={} if first else {5: 2, 6: 3},
        compiler_params=pltpu.CompilerParams(vmem_limit_bytes=VMEM_LIMIT),
        name="feed",
    )(*args)


def swap(value, axis, size, bit):
    return lax.ppermute(value, axis, [(d, d ^ bit) for d in range(size)])


def factors_of(size):
    found, stride = [], 1
    while stride < size:
        factor = 2 if stride == 1 or size // stride < 4 else 4
        found.append((factor, stride))
        stride *= factor
    return found


def chunk_of(value, index, count):
    rows = value.shape[0] // count
    return lax.dynamic_slice_in_dim(value, index * rows, rows, 0)


def scatter_stages(value, size):
    index = lax.axis_index("dp")
    for factor, stride in factors_of(size):
        mine = (index // stride) % factor
        sent = [chunk_of(value, mine ^ r, factor).astype(BF) for r in range(1, factor)]
        kept = chunk_of(value, mine, factor)
        sent, kept = yield sent, kept
        arrived = [swap(s, "dp", size, (r + 1) * stride) for r, s in enumerate(sent)]
        for piece in arrived:
            kept = kept + piece.astype(F32)
        value = kept
    piece = value.astype(BF)
    for factor, stride in reversed(factors_of(size)):
        mine = (index // stride) % factor
        sent, _ = yield [piece], None
        piece = sent[0]
        pieces = [piece] + [swap(piece, "dp", size, r * stride) for r in range(1, factor)]
        piece = jnp.concatenate(in_order(pieces, mine), axis=0)
    yield None, piece


class Chain:
    def __init__(self, value, size):
        self.steps = scatter_stages(value, size)
        self.sent, self.kept = next(self.steps)

    def tie(self, token):
        if self.sent is None:
            return token
        if self.kept is None:
            token, self.sent = lax.optimization_barrier((token, self.sent))
        else:
            token, self.sent, self.kept = lax.optimization_barrier((token, self.sent, self.kept))
        return token

    def advance(self):
        if self.sent is not None:
            self.sent, self.kept = self.steps.send((self.sent, self.kept))

    def finish(self):
        while self.sent is not None:
            self.advance()
        return self.kept


def in_order(pieces, mine):
    bit = 1
    while bit < len(pieces):
        on = (mine & bit) > 0
        pieces = [jnp.where(on, pieces[k ^ bit], pieces[k]) for k in range(len(pieces))]
        bit *= 2
    return pieces


class Flow:
    def __init__(self, rows, sums, quarters, groups):
        self.rows, self.sums, self.quarters = rows, sums, quarters
        self.stages = [("tensor", 4, 1), ("tensor", 4, 2)]
        self.stages += [("dp", groups, 1 << k) for k in range(groups.bit_length() - 1)]

    def tie(self, token):
        token, self.rows, self.sums = lax.optimization_barrier((token, self.rows, self.sums))
        return token

    def advance(self):
        if not self.stages:
            return
        axis, size, bit = self.stages.pop(0)
        rows, sums, quarters = self.rows, self.sums, self.quarters
        count, width = rows.shape
        flat = [rows.reshape(1, count * width), sums]
        if quarters is not None:
            flat += quarters[1::2] if len(quarters) > 1 else quarters
        came = swap(jnp.concatenate(flat, axis=1), axis, size, bit)
        rest = came[:, count * width :]
        came_rows = came[:, : count * width].reshape(count, width)
        on = (lax.axis_index(axis) & bit) > 0
        self.rows = jnp.concatenate(
            [jnp.where(on, came_rows, rows), jnp.where(on, rows, came_rows)], axis=0
        )
        if quarters is not None:
            span = quarters[0].shape[1]
            tail = rest[:, sums.shape[1] :]
            self.quarters = [
                q + tail[:, k * span : (k + 1) * span] for k, q in enumerate(quarters[0::2])
            ]
        self.sums = sums + rest[:, : sums.shape[1]]

    def finish(self):
        while self.stages:
            self.advance()
        return self.rows, self.sums, self.quarters


def tie(token, value):
    return lax.optimization_barrier((token, value))


def normed(values):
    center = values - jnp.mean(values, axis=-1, keepdims=True)
    variance = jnp.mean(center * center, axis=-1, keepdims=True)
    inverse = lax.rsqrt(variance + EPS)
    return center * inverse, inverse


def norm_back(grad, n, inverse, gain, scale):
    u = grad * (1.0 + scale) * gain
    return inverse * (
        u - jnp.mean(u, axis=-1, keepdims=True) - n * jnp.mean(u * n, axis=-1, keepdims=True)
    )


def rotary(length):
    half = HEAD_DIM // 2
    frequency = jnp.exp(jnp.arange(half, dtype=F32) * (-2.0 * math.log(10000.0) / HEAD_DIM))
    angles = frequency[:, None] * jnp.arange(length, dtype=jnp.int32).astype(F32)[None, :]
    return jnp.cos(angles), jnp.sin(angles)


def exact(left, right, contract):
    return lax.dot_general(
        left,
        right,
        (contract, ((), ())),
        precision=lax.Precision.HIGHEST,
        preferred_element_type=F32,
    )


def per_device(
    groups,
    tokens,
    cotangent,
    span_start,
    span_length,
    timestep,
    cond_table,
    mask_embed,
    ada_weight,
    ada_bias,
    first_gain,
    qkv_weight,
    out_weight,
    second_gain,
    up_weight,
    up_bias,
    down_weight,
    down_bias,
):
    _, length, width = tokens.shape
    packed = jnp.concatenate(
        [out_weight, jnp.broadcast_to(up_bias[None, :], (16, up_bias.shape[0]))], axis=0
    )
    bias_block = out_weight.shape[0] // 16

    own_qkv = qkv_weight.T
    wqkv = [own_qkv, swap(own_qkv, "tensor", 4, 1), swap(own_qkv, "tensor", 4, 2), None]
    wout = [packed, swap(packed, "tensor", 4, 1), swap(packed, "tensor", 4, 2), None]
    wup = [up_weight, swap(up_weight, "tensor", 4, 1), None, None]
    wdown = [down_weight, swap(down_weight, "tensor", 4, 1), None, None]

    cos, sin = rotary(length)
    raw = lax.dynamic_slice_in_dim(cond_table, timestep[0], 1, 0)
    sig = jax.nn.sigmoid(raw)
    condition = raw * sig
    modulation = jnp.sum(condition.T * ada_weight, axis=0, keepdims=True) + ada_bias[None, :]
    shift_one, scale_one, gate_one, shift_two, scale_two, gate_two = jnp.split(modulation, 6, axis=1)
    positions = jnp.arange(length, dtype=jnp.int32)[:, None]
    masked = (positions >= span_start[0]) & (positions < span_start[0] + span_length[0])
    start_rows = jnp.where(masked, mask_embed[None, :], tokens[0].astype(F32))
    n_one, inverse_one = normed(start_rows)
    first_low = (n_one * first_gain[None, :] * (1.0 + scale_one) + shift_one).astype(BF)

    attention_out = None
    kept = []
    for j in range(4):
        qkv, mixed, lse, attention_out = attend_forward(
            first_low, wqkv[j], wout[j], cos, sin, attention_out
        )
        if j == 0:
            lse, (wqkv[2], wout[2], up_weight) = tie(lse, (wqkv[2], wout[2], up_weight))
            wqkv[3] = swap(wqkv[2], "tensor", 4, 1)
            wout[3] = swap(wout[2], "tensor", 4, 1)
            wup[2] = swap(up_weight, "tensor", 4, 2)
        if j == 1:
            lse, down_weight = tie(lse, down_weight)
            wdown[2] = swap(down_weight, "tensor", 4, 2)
        if j == 3:
            lse, wup[2] = tie(lse, wup[2])
            wup[3] = swap(wup[2], "tensor", 4, 1)
        kept.append((qkv, mixed, lse))

    middle = start_rows + gate_one * attention_out
    n_two, inverse_two = normed(middle)
    second_low = (n_two * second_gain[None, :] * (1.0 + scale_two) + shift_two).astype(BF)
    upstream = cotangent[0].astype(F32)
    feed_grad = (gate_two * upstream).astype(BF)

    carried = None
    feed_parts, bias_parts = [None] * 4, [None] * 4
    for j in (0, 3, 2, 1):
        part, bias_part, *carried = feed(
            second_low, feed_grad, wup[j], wdown[j], wout[j], bias_block, carried
        )
        feed_parts[j] = part.reshape(2 * part.shape[1], width)
        bias_parts[j] = bias_part[0:1]
        if j == 0:
            bias_parts[0], wdown[2] = tie(bias_parts[0], wdown[2])
            wdown[3] = swap(wdown[2], "tensor", 4, 1)
        if j == 2:
            feed_other = (feed_parts[2] + swap(feed_parts[3], "tensor", 4, 1)).astype(BF)
            wup[1], feed_other = tie(wup[1], feed_other)
            feed_across = swap(feed_other, "tensor", 4, 2)
    feed_sum, second_grad = carried
    feed_out = feed_sum + down_bias.astype(F32)[None, :]
    layer_out = (middle + gate_two * feed_out).astype(BF)
    gate_two_grad = jnp.sum(upstream * feed_out, axis=0, keepdims=True)
    down_bias_grad = jnp.sum(feed_grad.astype(F32), axis=0, keepdims=True)
    shift_two_grad = jnp.sum(second_grad, axis=0, keepdims=True)
    product_two = jnp.sum(second_grad * n_two, axis=0, keepdims=True)
    scale_two_grad = product_two * second_gain[None, :]
    second_gain_grad = product_two * (1.0 + scale_two)
    middle_grad = upstream + norm_back(
        second_grad, n_two, inverse_two, second_gain[None, :], scale_two
    )
    gate_one_grad = jnp.sum(middle_grad * attention_out, axis=0, keepdims=True)
    attention_grad = (gate_one * middle_grad).astype(BF)
    early = Flow(
        jnp.concatenate(
            [
                gate_one_grad,
                shift_two_grad,
                scale_two_grad,
                gate_two_grad,
                condition,
                jnp.broadcast_to(timestep.astype(F32)[:, None], (1, 128)),
            ],
            axis=1,
        ),
        jnp.concatenate([second_gain_grad, down_bias_grad], axis=1),
        bias_parts,
        groups,
    )

    first_grad = None
    parts = [None] * 4
    lses = {j: kept[j][2] for j in range(4)}
    for j in (3, 2, 1, 0):
        parts[j], first_grad = attend_backward(
            first_low, attention_grad, wqkv[j], wout[j], *kept[j][:2], lses[j], cos, sin, first_grad
        )
        first_grad, parts[j] = tie(first_grad, parts[j])
        if j == 3:
            feed_chain = Chain(
                feed_parts[0] + swap(feed_parts[1], "tensor", 4, 1) + feed_across.astype(F32), groups
            )
        else:
            feed_chain.advance()
        early.advance()
        if j == 2:
            other = (parts[2] + swap(parts[3], "tensor", 4, 1)).astype(BF)
            lses[1], other = tie(lses[1], other)
            across = swap(other, "tensor", 4, 2)
        if j > 0:
            lses[j - 1] = early.tie(feed_chain.tie(lses[j - 1]))
    chain = Chain(parts[0] + swap(parts[1], "tensor", 4, 1) + across.astype(F32), groups)
    first_grad = chain.tie(first_grad)
    chain.advance()
    feed_final = feed_chain.finish().astype(F32)
    early_rows, early_sums, early_quarter = early.finish()

    shift_one_grad = jnp.sum(first_grad, axis=0, keepdims=True)
    product_one = jnp.sum(first_grad * n_one, axis=0, keepdims=True)
    scale_one_grad = product_one * first_gain[None, :]
    first_gain_grad = product_one * (1.0 + scale_one)
    start_grad = middle_grad + norm_back(
        first_grad, n_one, inverse_one, first_gain[None, :], scale_one
    )
    tokens_grad = jnp.where(masked, 0.0, start_grad)[None]
    mask_grad = jnp.sum(jnp.where(masked, start_grad, 0.0), axis=0, keepdims=True)

    own_modulation = jnp.concatenate(
        [shift_one_grad, scale_one_grad, gate_one_grad, shift_two_grad, scale_two_grad, gate_two_grad],
        axis=1,
    )
    cond_grad = jnp.sum(ada_weight * own_modulation, axis=1)[None, :]
    cond_grad = cond_grad * (sig * (1.0 + raw * (1.0 - sig)))
    late = Flow(
        jnp.concatenate([shift_one_grad, scale_one_grad, cond_grad], axis=1),
        jnp.concatenate([mask_grad, first_gain_grad], axis=1),
        None,
        groups,
    )
    while late.stages:
        late.rows = chain.tie(late.rows)
        late.advance()
        chain.advance()
    late_rows, late_sums, _ = late.finish()
    attention_final = chain.finish().astype(F32)

    conditions = early_rows[:, 4 * width : 4 * width + 128]
    steps = early_rows[:, 4 * width + 128 : 4 * width + 129].astype(jnp.int32)
    all_modulation = jnp.concatenate([late_rows[:, : 2 * width], early_rows[:, : 4 * width]], axis=1)
    ada_weight_grad = exact(conditions, all_modulation, ((0,), (0,)))
    ada_bias_grad = jnp.sum(all_modulation, axis=0)
    chosen = (steps == jnp.arange(cond_table.shape[0], dtype=jnp.int32)[None, :]).astype(F32)
    table_grad = exact(chosen, late_rows[:, 2 * width :], ((0,), (0,)))

    units = up_weight.shape[1]
    heads_rows = qkv_weight.shape[1]
    return (
        layer_out[None],
        tokens_grad,
        table_grad,
        late_sums[0, :width],
        ada_weight_grad,
        ada_bias_grad,
        late_sums[0, width:],
        attention_final[:heads_rows].T,
        attention_final[heads_rows:],
        early_sums[0, :width],
        feed_final[:units].T,
        early_quarter[0][0],
        feed_final[units:],
        early_sums[0, width:],
    )


def solution(mesh):
    rows = P(("dp", "tensor"), None, None)
    each = P(("dp", "tensor"))
    columns = P(None, "tensor")
    lines = P("tensor", None)

    def body(*arrays):
        return per_device(mesh.shape["dp"], *arrays)

    return jax.shard_map(
        body,
        mesh=mesh,
        in_specs=(
            rows, rows, each, each, each, P(), P(), P(), P(), P(),
            columns, lines, P(), columns, P("tensor"), lines, P(),
        ),
        out_specs=(
            rows, rows, P(), P(), P(), P(), P(), columns, lines, P(),
            columns, P("tensor"), lines, P(),
        ),
        check_vma=False,
    )
```
